32 devices in a mesh: elem: 32 (over z, y, x, core).
Axes of the slice: x: 2, y: 2, z: 4, core: 2. Of those that a mesh axis runs over, the one named last changes fastest.
Arguments:
- tracers: float32 [512, 4, 16, 128], P('elem'), may hold values from -6 to 6
- sources: float32 [512, 4, 16, 128], P('elem'), may hold values from -3 to 3
- weights: float32 [512, 4, 256], P('elem'), may hold values from -0.3 to 0.425
- dep_owner: int32 [512, 4, 16], P('elem'), may hold values from 0 to 31, as said below
- dep_slot: int32 [512, 4, 16], P('elem'), may hold values from 0 to 15, as said below
- nbr_elem: int32 [512, 4], P('elem'), may hold values from 0 to 511, as said below
- nbr_edge: int32 [512, 4], P('elem'), may hold values from 0 to 3, as said below
- metric: float32 [512, 2, 16], P('elem'), may hold values from 0.5 to 2
Outputs:
- settled: float32 [512, 4, 16, 128], P('elem')
The draws below stay inside these ranges and needn't reach their ends.
Inputs may be any that keep to these rules, and one draw needn't show every extreme that they name: `dep_owner`: the departure element of a target point is its own element or one of its four edge neighbours, so its owner is the point's own device or the one before or after it, cyclically. Of one device's target points at most 1024 have departure elements on the next device and at most 1024 on the previous one; each bound is reached on some device in every draw. `dep_slot`: together with dep_owner it names the departure element. `nbr_elem`: global index is owner times 16 plus position. Edges are listed counterclockwise; the relation is symmetric and no element is its own neighbour. Every neighbour lies on the same device or the one before or after it, cyclically; exactly 16 edges of one device's elements face the next device and exactly 16 the previous one. `nbr_edge`: the neighbour's entry for that edge points back to the element and edge.
All inputs are finite; a program needn't handle non-finite values.
Results may differ from the reference program's by a relative error of at most 0.0003.
Values sent between devices are 32-bit elements; how exact they have to be, the bound alone decides.
No kernel may reach another device: no remote copies, remote signals or barrier semaphores. Data moves between devices by JAX's collectives and lax.ppermute only.
A program may use at most 128 MiB of HBM per device.

```python
import math
import jax
import jax.numpy as jnp
import numpy as np
from jax import lax

GLL = 16
Q = 128
LEV = 4
BX = 16
EL_DEV = 16
ELEMS = 512


def element_mesh(key):
    base = jax.random.fold_in(key, 7)
    devices = ELEMS // EL_DEV
    rows_each = EL_DEV // BX
    total_rows = devices * rows_each
    device_keys = jax.random.split(jax.random.fold_in(base, 1), devices)
    layout = jax.vmap(lambda sub_key: jax.random.permutation(sub_key, EL_DEV))(device_keys).astype(jnp.int32)
    inverse = jnp.argsort(layout, axis=1).astype(jnp.int32)
    rotation = jax.random.randint(jax.random.fold_in(base, 2), (ELEMS,), 0, 4, dtype=jnp.int32)
    owner_dev = jnp.arange(ELEMS, dtype=jnp.int32) // EL_DEV
    grid_cell = layout.reshape(-1)
    grid_row = owner_dev * rows_each + grid_cell // BX
    grid_col = grid_cell % BX
    row_step = jnp.array([-1, 0, 1, 0], jnp.int32)
    col_step = jnp.array([0, 1, 0, -1], jnp.int32)
    new_row = (grid_row[:, None] + row_step[None, :]) % total_rows
    new_col = (grid_col[:, None] + col_step[None, :]) % BX
    new_owner = new_row // rows_each
    new_cell = new_row % rows_each * BX + new_col
    by_direction = new_owner * EL_DEV + inverse[new_owner, new_cell]
    return (by_direction, rotation)


def neighbour_lists(key):
    by_direction, rotation = element_mesh(key)
    sides = jnp.arange(4, dtype=jnp.int32)
    direction = (sides[None, :] + rotation[:, None]) % 4
    across = jnp.take_along_axis(by_direction, direction, axis=1)
    back_dir = (direction + 2) % 4
    their_edge = (back_dir - rotation[across]) % 4
    return (across.astype(jnp.int32), their_edge.astype(jnp.int32))


def departures(key):
    by_direction, rotation = element_mesh(key)
    devices = ELEMS // EL_DEV
    base = jax.random.fold_in(key, 19)
    upward = jax.random.randint(jax.random.fold_in(base, 1), (devices,), 1, 11, dtype=jnp.int32)
    downward = jax.random.randint(jax.random.fold_in(base, 2), (devices,), 1, 11, dtype=jnp.int32)
    forced_up = jax.random.randint(jax.random.fold_in(base, 3), (), 0, devices, dtype=jnp.int32)
    forced_down = (forced_up + 1 + jax.random.randint(jax.random.fold_in(base, 4), (), 0, devices - 1, dtype=jnp.int32)) % devices
    device_ids = jnp.arange(devices, dtype=jnp.int32)
    upward = jnp.where(device_ids == forced_up, 20, jnp.where(device_ids == forced_down, 0, upward))
    downward = jnp.where(device_ids == forced_down, 20, jnp.where(device_ids == forced_up, 0, downward))
    throws = jax.random.randint(jax.random.fold_in(base, 5), (ELEMS, LEV, GLL), 0, 20, dtype=jnp.int32)
    owner_dev = jnp.arange(ELEMS, dtype=jnp.int32) // EL_DEV
    up_share = upward[owner_dev][:, None, None]
    down_share = downward[owner_dev][:, None, None]
    remainder = throws % 3
    grid_dir = jnp.where(throws < up_share, 2, jnp.where(throws < up_share + down_share, 0, jnp.where(remainder == 0, -1, jnp.where(remainder == 1, 1, 3))))
    self_ids = jnp.broadcast_to(jnp.arange(ELEMS, dtype=jnp.int32)[:, None, None], (ELEMS, LEV, GLL))
    chosen = jnp.where(grid_dir < 0, self_ids, by_direction[self_ids, jnp.maximum(grid_dir, 0)])
    return ((chosen // EL_DEV).astype(jnp.int32), (chosen % EL_DEV).astype(jnp.int32))


def draw_dep_owner(key, part):
    return departures(key)[0]


def draw_dep_slot(key, part):
    return departures(key)[1]


def draw_nbr_elem(key, part):
    return neighbour_lists(key)[0]


def draw_nbr_edge(key, part):
    return neighbour_lists(key)[1]


def level_of(stream_key, extent, cuts, smallest, high):
    gain = 1.0
    for position, parts in cuts:
        heights = jax.random.uniform(jax.random.fold_in(jax.random.fold_in(stream_key, 6), position), (parts,), jnp.float32, smallest / len(cuts), high / len(cuts))
        gain = gain * jnp.repeat(jnp.exp(heights), extent[position] // parts).reshape((-1,) + (1,) * (len(extent) - 1 - position))
    return gain


def centred(stream_key, shape, width, bound, pieces=(), held_as=jnp.bfloat16):
    level = level_of(stream_key, shape, pieces, -0.22, 0.18) if pieces else 1.0
    drawn = jax.random.normal(stream_key, shape, jnp.float32) * width * level
    return jnp.minimum(jnp.maximum(drawn, -bound), bound).astype(held_as)


def setup_inputs(seed: int = 0) -> dict:
    key_of = jax.random.split(jax.random.key(seed), 9)
    tracers = centred(key_of[0], (ELEMS, LEV, GLL, Q), 1.0, 6.0, ((0, 32),), jnp.float32)
    sources = centred(key_of[1], (ELEMS, LEV, GLL, Q), 0.5, 3.0, ((0, 32),), jnp.float32)
    weights = jnp.clip(-0.3 + 0.725 * jax.random.uniform(key_of[2], (ELEMS, LEV, GLL * GLL), jnp.float32) ** level_of(key_of[2], (ELEMS, LEV, GLL * GLL), ((0, 32),), -0.2, 0.2), -0.3, 0.425)
    dep_owner = draw_dep_owner(jax.random.fold_in(key_of[8], 71), 0)
    dep_slot = draw_dep_slot(jax.random.fold_in(key_of[8], 71), 0)
    nbr_elem = draw_nbr_elem(jax.random.fold_in(key_of[8], 71), 0)
    nbr_edge = draw_nbr_edge(jax.random.fold_in(key_of[8], 71), 0)
    metric = jnp.clip(jnp.exp(math.log(2.0) - 1.3862944 * jax.random.uniform(key_of[7], (ELEMS, 2, GLL), jnp.float32) ** level_of(key_of[7], (ELEMS, 2, GLL), ((0, 32),), -0.2, 0.2)), 0.5, 2.0)
    return dict(tracers=tracers, sources=sources, weights=weights, dep_owner=dep_owner, dep_slot=dep_slot, nbr_elem=nbr_elem, nbr_edge=nbr_edge, metric=metric)


VISCOSITY = 0.002
HIGH = lax.Precision.HIGHEST

def gll_tables():
    gll_nodes = np.array([-1.0, -np.sqrt(0.2), np.sqrt(0.2), 1.0])
    node_count = gll_nodes.shape[0]
    bary_weights = np.array([1.0 / np.prod([gll_nodes[j] - gll_nodes[m] for m in range(node_count) if m != j]) for j in range(node_count)])
    derivative = np.zeros((node_count, node_count))
    for i in range(node_count):
        for j in range(node_count):
            if i != j:
                derivative[i, j] = bary_weights[j] / bary_weights[i] / (gll_nodes[i] - gll_nodes[j])
        derivative[i, i] = -np.sum(derivative[i])
    identity = np.eye(node_count)
    along_a = np.kron(derivative, identity)
    along_b = np.kron(identity, derivative)
    edge_points = np.array([[4 * k for k in range(4)], [12 + k for k in range(4)], [4 * (3 - k) + 3 for k in range(4)], [3 - k for k in range(4)]], dtype=np.int32)
    spread = np.zeros((4, 4, 16))
    for s in range(4):
        for k in range(4):
            spread[s, k, edge_points[s, k]] = 1.0
    counts = 1.0 + spread.sum(axis=(0, 1))
    return (along_a, along_b, edge_points, spread, counts)

def interpolate(source_table, rows_from, block_weights):
    level_count = rows_from.shape[1]
    points = rows_from.shape[2]
    shaped = block_weights.reshape(block_weights.shape[0], level_count, points, points)
    levels_out = []
    for level in range(level_count):
        gathered = source_table[rows_from[:, level], level]
        levels_out.append(lax.optimization_barrier(jnp.sum(shaped[:, level][..., None] * gathered, axis=2)))
    return jnp.stack(levels_out, axis=1)

def local_laplacian(field_in, metric, tables):
    along_a = jnp.asarray(tables[0], field_in.dtype)
    along_b = jnp.asarray(tables[1], field_in.dtype)
    grad_a = jnp.einsum('pm,elmq->elpq', along_a, field_in, precision=HIGH)
    grad_b = jnp.einsum('pm,elmq->elpq', along_b, field_in, precision=HIGH)
    flux_a = metric[:, 0][:, None, :, None] * grad_a
    flux_b = metric[:, 1][:, None, :, None] * grad_b
    return jnp.einsum('pm,elmq->elpq', along_a, flux_a, precision=HIGH) + jnp.einsum('pm,elmq->elpq', along_b, flux_b, precision=HIGH)

def partner_edges(gathered, facing_edge, tables):
    reversed_points = jnp.asarray(tables[2][:, ::-1].copy(), jnp.int32)
    pick = (facing_edge[..., None] == jnp.arange(4, dtype=jnp.int32)).astype(jnp.int32)
    wanted = lax.optimization_barrier(jnp.sum(pick[..., None] * reversed_points, axis=2))
    select = (wanted[..., None] == jnp.arange(gathered.shape[3], dtype=jnp.int32)).astype(gathered.dtype)
    return jnp.einsum('eskp,eslpq->eslkq', select, gathered, precision=HIGH)

def close_edges(field_in, received, tables):
    spread = jnp.asarray(tables[3], field_in.dtype)
    counts = jnp.asarray(tables[4], field_in.dtype)
    added = jnp.einsum('skp,eslkq->elpq', spread, received, precision=HIGH)
    return (field_in + added) / counts[None, None, :, None]

def advect(field_in, dep_owner, dep_slot, weights):
    where_from = dep_owner * EL_DEV + dep_slot
    blocks = field_in.shape[0] // EL_DEV

    def one_block(block):
        start = block * EL_DEV
        rows_from = lax.dynamic_slice_in_dim(where_from, start, EL_DEV, 0)
        block_weights = lax.dynamic_slice_in_dim(weights, start, EL_DEV, 0)
        return interpolate(field_in, rows_from, block_weights)
    return lax.map(one_block, jnp.arange(blocks, dtype=jnp.int32)).reshape(field_in.shape)

def edge_close(field_in, nbr_elem, nbr_edge, tables):
    blocks = field_in.shape[0] // EL_DEV

    def one_block(block):
        start = block * EL_DEV
        own_values = lax.dynamic_slice_in_dim(field_in, start, EL_DEV, 0)
        partner = lax.dynamic_slice_in_dim(nbr_elem, start, EL_DEV, 0)
        facing = lax.dynamic_slice_in_dim(nbr_edge, start, EL_DEV, 0)
        received = partner_edges(field_in[partner], facing, tables)
        return close_edges(own_values, received, tables)
    return lax.map(one_block, jnp.arange(blocks, dtype=jnp.int32)).reshape(field_in.shape)

def reference(tracers, sources, weights, dep_owner, dep_slot, nbr_elem, nbr_edge, metric):
    tables = gll_tables()
    first = advect(tracers, dep_owner, dep_slot, weights) + sources
    second = advect(first, dep_owner, dep_slot, weights) + sources
    lap_once = edge_close(local_laplacian(second, metric, tables), nbr_elem, nbr_edge, tables)
    lap_twice = edge_close(local_laplacian(lap_once, metric, tables), nbr_elem, nbr_edge, tables)
    return second - VISCOSITY * lap_twice
```

```python
import functools

import jax
import jax.numpy as jnp
import numpy as np
from jax import lax
from jax.experimental import pallas as pl
from jax.experimental.pallas import tpu as pltpu
from jax.sharding import PartitionSpec as P

VISCOSITY = 0.002
HIGH = lax.Precision.HIGHEST
F32 = jnp.float32
BF16 = jnp.bfloat16
VM = pl.BlockSpec(memory_space=pltpu.VMEM)
PARAMS = pltpu.CompilerParams(vmem_limit_bytes=24 * 1024 * 1024)


def gll_tables():
    nodes = np.array([-1.0, -np.sqrt(0.2), np.sqrt(0.2), 1.0])
    m = nodes.shape[0]
    bary = np.array(
        [1.0 / np.prod([nodes[j] - nodes[i] for i in range(m) if i != j]) for j in range(m)]
    )
    deriv = np.zeros((m, m))
    for i in range(m):
        for j in range(m):
            if i != j:
                deriv[i, j] = bary[j] / bary[i] / (nodes[i] - nodes[j])
        deriv[i, i] = -np.sum(deriv[i])
    along_a = np.kron(deriv, np.eye(m))
    along_b = np.kron(np.eye(m), deriv)
    edge_points = np.array(
        [
            [4 * k for k in range(4)],
            [12 + k for k in range(4)],
            [4 * (3 - k) + 3 for k in range(4)],
            [3 - k for k in range(4)],
        ],
        dtype=np.int32,
    )
    return along_a, along_b, edge_points


def split(x):
    hi = x.astype(BF16)
    lo = (x - hi.astype(F32)).astype(BF16)
    return hi, lo


def mm(a, b):
    return jnp.dot(a, b, preferred_element_type=F32)


def mm3(a_hi, a_lo, x):
    x_hi, x_lo = split(x)
    return mm(a_hi, x_hi) + (mm(a_hi, x_lo) + mm(a_lo, x_hi))


def iota(shape, dim):
    return lax.broadcasted_iota(jnp.int32, shape, dim)


def inverse_counts(shape, points):
    p = iota(shape, 0) % points
    a, b = p // 4, p % 4
    hits = [(v == end).astype(F32) for v in (a, b) for end in (0, 3)]
    return 1.0 / (1.0 + hits[0] + hits[1] + hits[2] + hits[3])


def prep_kernel(w_ref, cols_ref, metric_ref, a_ref, b_ref, mhi_ref, mlo_ref, ghi_ref, glo_ref, u_ref):
    elements, levels, squared = w_ref.shape
    rows = cols_ref.shape[0]
    points = rows // elements
    faces = u_ref.shape[1]
    row_point = iota((rows, squared), 0) % points
    own_group = iota((rows, squared), 1) // points == row_point
    tile = (iota((squared, rows), 0) % points == iota((squared, rows), 1) % points).astype(BF16)
    lane_element = iota((rows, rows), 1) // points
    for k in range(levels):
        spread = jnp.broadcast_to(w_ref[:, k, :][:, None, :], (elements, points, squared))
        spread = jnp.where(own_group, spread.reshape(rows, squared), 0.0)
        hi, lo = split(spread)
        hi, lo = mm(hi, tile), mm(lo, tile)
        code = cols_ref[:, k : k + 1]
        for side in range(3):
            match = lane_element + side * elements == code
            at = pl.ds(side * rows, rows)
            mhi_ref[k, :, at] = jnp.where(match, hi, 0.0).astype(BF16)
            mlo_ref[k, :, at] = jnp.where(match, lo, 0.0).astype(BF16)
    local = jnp.dot(a_ref[...] * metric_ref[0:1, :], a_ref[...], precision=HIGH) + jnp.dot(
        b_ref[...] * metric_ref[1:2, :], b_ref[...], precision=HIGH
    )
    lane = iota((rows, rows + faces), 1)
    links = jnp.zeros((rows, rows + faces), F32)
    for s in range(4):
        links = links + (lane == cols_ref[:, levels + s : levels + s + 1]).astype(F32)
    eye = (iota((rows, rows), 0) == iota((rows, rows), 1)).astype(F32)
    closed = jnp.dot(links[:, :rows] + eye, local, precision=HIGH)
    sent = lax.dot_general(
        links[:, rows:], local, (((0,), (0,)), ((), ())), precision=HIGH, preferred_element_type=F32
    )
    ghi_ref[:rows, :], glo_ref[:rows, :] = split(closed)
    ghi_ref[rows:, :], glo_ref[rows:, :] = split(sent)
    u_ref[...] = links[:, rows:].astype(BF16)


def level_of(ref, k):
    x = ref[:, k]
    return x.reshape(x.shape[0] * x.shape[1], x.shape[2])


def advect_level(mhi_ref, mlo_ref, parts, k):
    rows = mhi_ref.shape[1]
    total = None
    for side, ref in parts:
        at = pl.ds(side * rows, rows)
        term = mm3(mhi_ref[k, :, at], mlo_ref[k, :, at], level_of(ref, k))
        total = term if total is None else total + term
    return total


def advect_kernel(mhi_ref, mlo_ref, own_ref, near_ref, far_ref, src_ref, out_ref):
    for k in range(own_ref.shape[1]):
        parts = ((0, own_ref), (1, near_ref), (2, far_ref))
        x = advect_level(mhi_ref, mlo_ref, parts, k) + level_of(src_ref, k)
        out_ref[:, k] = x.reshape(out_ref.shape[0], -1, x.shape[1])


def emit_edges(ghi_ref, glo_ref, fields, part_ref, near_ref, far_ref):
    width = fields[0].shape[1]
    rows = fields[0].shape[0]
    half = near_ref.shape[1]
    y = mm3(ghi_ref[...], glo_ref[...], jnp.concatenate(fields, axis=1))
    for k in range(len(fields)):
        at = slice(k * width, (k + 1) * width)
        part_ref[k] = y[:rows, at]
        near_ref[k] = y[rows : rows + half, at]
        far_ref[k] = y[rows + half :, at]


def second_kernel(
    mhi_ref, mlo_ref, ghi_ref, glo_ref, own_ref, near_ref, far_ref, src_ref,
    second_ref, part_ref, near_out_ref, far_out_ref,
):
    fields = []
    for k in range(own_ref.shape[1]):
        parts = ((0, own_ref), (1, near_ref), (2, far_ref))
        x = advect_level(mhi_ref, mlo_ref, parts, k) + level_of(src_ref, k)
        second_ref[k] = x
        fields.append(x)
    emit_edges(ghi_ref, glo_ref, fields, part_ref, near_out_ref, far_out_ref)


def closed_level(u_ref, part_ref, near_ref, far_ref, scale, k):
    hi, lo = split(jnp.concatenate([near_ref[k], far_ref[k]], axis=0))
    return (part_ref[k] + mm(u_ref[...], hi) + mm(u_ref[...], lo)) * scale


def once_kernel(u_ref, ghi_ref, glo_ref, part_ref, near_ref, far_ref, part_out_ref, near_out_ref, far_out_ref):
    levels, rows, width = part_ref.shape
    scale = inverse_counts((rows, width), 16)
    fields = [closed_level(u_ref, part_ref, near_ref, far_ref, scale, k) for k in range(levels)]
    emit_edges(ghi_ref, glo_ref, fields, part_out_ref, near_out_ref, far_out_ref)


def settle_kernel(u_ref, part_ref, near_ref, far_ref, second_ref, out_ref):
    levels, rows, width = part_ref.shape
    scale = inverse_counts((rows, width), 16) * VISCOSITY
    for k in range(levels):
        x = second_ref[k] - closed_level(u_ref, part_ref, near_ref, far_ref, scale, k)
        out_ref[:, k] = x.reshape(out_ref.shape[0], -1, width)


def call(kernel, outs, *args):
    return pl.pallas_call(
        kernel,
        out_shape=outs,
        in_specs=[VM] * len(args),
        out_specs=jax.tree.map(lambda _: VM, outs),
        compiler_params=PARAMS,
    )(*args)


def columns(dep_owner, dep_slot, nbr_elem, nbr_edge, me, near, far, edge_points):
    elements, levels, points = dep_owner.shape
    side = jnp.where(dep_owner == me, 0, jnp.where(dep_owner == near, 1, 2))
    code = side * elements + dep_slot
    code = code.transpose(0, 2, 1).reshape(elements * points, levels)

    owner, slot = nbr_elem // elements, nbr_elem % elements
    sides = jnp.where(owner == me, 0, jnp.where(owner == near, 1, 2))
    mine = lax.broadcasted_iota(jnp.int32, nbr_elem.shape, 0) * 4 + lax.broadcasted_iota(
        jnp.int32, nbr_elem.shape, 1
    )
    leads = jnp.where(sides == 1, me % 2 == 0, me % 2 == 1)
    key = jnp.where(leads, mine, slot * 4 + nbr_edge)
    before = (sides[:, :, None, None] == sides[None, None]) & (key[None, None] < key[:, :, None, None])
    rank = jnp.sum(before.astype(jnp.int32), axis=(2, 3))

    place = -np.ones((points, 4), np.int32)
    for s in range(4):
        for k in range(4):
            place[edge_points[s, k], s] = k
    flipped = np.where(place >= 0, 3 - place, 0)
    partner = np.stack([edge_points[t][flipped] for t in range(4)])
    edge = nbr_edge[:, None, :]
    their = jnp.where(
        edge == 0, partner[0], jnp.where(edge == 1, partner[1], jnp.where(edge == 2, partner[2], partner[3]))
    )
    at = jnp.where(leads[:, None, :], place, flipped)
    rows = elements * points
    index = jnp.where(
        sides[:, None, :] == 0,
        slot[:, None, :] * points + their,
        rows + (sides[:, None, :] - 1) * (4 * elements) + rank[:, None, :] * 4 + at,
    )
    index = jnp.where(place >= 0, index, -1).reshape(rows, 4)
    return jnp.concatenate([code, index], axis=1)


def local(tracers, sources, weights, dep_owner, dep_slot, nbr_elem, nbr_edge, metric):
    along_a, along_b, edge_points = gll_tables()
    elements, levels, points, width = tracers.shape
    rows = elements * points
    half = 4 * elements
    devices = lax.axis_size("elem")
    me = lax.axis_index("elem")
    odd = me % 2
    near = me + 1 - 2 * odd
    far = (me - 1 + 2 * odd + devices) % devices
    near_pairs = [(i, i ^ 1) for i in range(devices)]
    far_pairs = [(i, (i - 1 + 2 * (i % 2)) % devices) for i in range(devices)]

    def swap(to_near, to_far):
        from_far = lax.ppermute(to_far, "elem", far_pairs)
        from_near = lax.ppermute(to_near, "elem", near_pairs)
        return from_near, from_far

    shape = jax.ShapeDtypeStruct
    t_near, t_far = swap(tracers, tracers)
    cols = columns(dep_owner, dep_slot, nbr_elem, nbr_edge, me, near, far, edge_points)
    metric_rows = metric.transpose(1, 0, 2).reshape(2, rows)
    eye = np.eye(elements)
    big_a = jnp.asarray(np.kron(eye, along_a), F32)
    big_b = jnp.asarray(np.kron(eye, along_b), F32)
    mhi, mlo, ghi, glo, u = call(
        prep_kernel,
        (
            shape((levels, rows, 3 * rows), BF16),
            shape((levels, rows, 3 * rows), BF16),
            shape((rows + 2 * half, rows), BF16),
            shape((rows + 2 * half, rows), BF16),
            shape((rows, 2 * half), BF16),
        ),
        weights, cols, metric_rows, big_a, big_b,
    )
    first = call(advect_kernel, shape(tracers.shape, F32), mhi, mlo, tracers, t_near, t_far, sources)
    f_near, f_far = swap(first, first)
    whole = shape((levels, rows, width), F32)
    edges = shape((levels, half, width), F32)
    second, part, x_near, x_far = call(
        second_kernel, (whole, whole, edges, edges), mhi, mlo, ghi, glo, first, f_near, f_far, sources
    )
    x_near, x_far = swap(x_near, x_far)
    part, x_near, x_far = call(once_kernel, (whole, edges, edges), u, ghi, glo, part, x_near, x_far)
    x_near, x_far = swap(x_near, x_far)
    return call(settle_kernel, shape(tracers.shape, F32), u, part, x_near, x_far, second)


def solution(mesh):
    placed = (
        P("elem", None, None, None),
        P("elem", None, None, None),
        P("elem", None, None),
        P("elem", None, None),
        P("elem", None, None),
        P("elem", None),
        P("elem", None),
        P("elem", None, None),
    )
    return jax.shard_map(
        local, mesh=mesh, in_specs=placed, out_specs=P("elem", None, None, None), check_vma=False
    )
```
